256 devices in a mesh: dp: 8 (over y, core), expert: 32 (over x, z).
Axes of the slice: x: 4, y: 4, z: 8, core: 2. Of those that a mesh axis runs over, the one named last changes fastest.
Arguments:
- tokens: bfloat16 [2048, 4096], P(('dp', 'expert')), may hold values from -6 to 6
- expert_ids: int32 [2048, 8], P(('dp', 'expert')), may hold values from 0 to 31, all different within a row; in each aligned block of 8 rows (0 to 7, 8 to 15, ...) at most 3 rows name the same one
- gate_values: float32 [2048, 8], P(('dp', 'expert')), may hold values from 0.05 to 1
- w_gate: bfloat16 [32, 4096, 2048], P('expert', None, 'dp'), may hold values from -0.09375 to 0.09375
- w_up: bfloat16 [32, 4096, 2048], P('expert', None, 'dp'), may hold values from -0.09375 to 0.09375
- w_down: bfloat16 [32, 2048, 4096], P('expert', 'dp'), may hold values from -0.125 to 0.125
- s_gate: bfloat16 [4096, 2048], P(None, 'dp'), may hold values from -0.09375 to 0.09375
- s_up: bfloat16 [4096, 2048], P(None, 'dp'), may hold values from -0.09375 to 0.09375
- s_down: bfloat16 [2048, 4096], P('dp'), may hold values from -0.125 to 0.125
Outputs:
- mixed: bfloat16 [2048, 4096], P(('dp', 'expert'))
The draws below stay inside these ranges and needn't reach their ends.
Inputs may be any that keep to these rules, and one draw needn't show every extreme that they name: `expert_ids`: each row names 8 different experts; the 8 rows of one device name one expert at most 3 times.
All inputs are finite; a program needn't handle non-finite values.
Results may differ from the reference program's by a relative error of at most 0.0054.
Values may be sent and summed in bfloat16 or wider, within the bound.
No kernel may reach another device: no remote copies, remote signals or barrier semaphores. Data moves between devices by JAX's collectives and lax.ppermute only.
A program may use at most 128 MiB of HBM per device.

```python
import math
import jax
import jax.numpy as jnp
import numpy as np
from jax import lax

D = 4096
FF = 2048
SFF = 2048
TOP = 8
TOK_DEV = 8
EXPERTS = 32
TOKENS = 2048
CAP = 3
N_DP = 8


def steps_of(key, shape, shards, least, top_value):
    def one(dim, shards_of):
        draws = jax.random.uniform(jax.random.fold_in(jax.random.fold_in(key, 6), dim), (shards_of,), jnp.float32, least / len(shards), top_value / len(shards))
        return jnp.repeat(jnp.exp(draws), shape[dim] // shards_of).reshape((-1,) + (1,) * (len(shape) - dim - 1))

    level = one(*shards[0])
    for cut in shards[1:]:
        level = level * one(*cut)
    return level


def deal_out(key, own, number, rows, number_of, top, reach, skew):
    ranking = jax.random.permutation(key, number_of)
    packed, common = load_shares(number_of, rows * top, reach, skew, True), load_shares(number_of, rows * top, reach, skew, False)
    places = jnp.arange(number_of)

    def named(sizes, turn):
        used = int((sizes > 0).sum())
        fixed = max(1, used // 4)
        moved = fixed + (places - fixed + turn * (used - fixed)) % max(1, number_of - fixed)
        return jnp.zeros((number_of,), jnp.int32).at[ranking[jnp.where(places < fixed, places, moved)]].set(jnp.asarray(sizes, jnp.int32))

    sizes = jnp.where(number % 4 == 0, named(packed, number // 4), named(common, number - number // 4 - 1))
    mixed = jax.random.permutation(jax.random.fold_in(own, 3), number_of)
    source_of, sink = mixed[0:number_of // 2 * 2:2], mixed[1:number_of // 2 * 2:2]
    margin = jnp.minimum(sizes[source_of] - 1, reach - sizes[sink]) // 2
    margin = jnp.where((source_of == ranking[0]) | (sink == ranking[0]) | (sizes[sink] == 0), 0, jnp.maximum(margin, 0))
    moved = jax.random.randint(jax.random.fold_in(own, 4), (number_of // 2,), 0, 1 << 20) % (margin + 1)
    sizes = sizes.at[source_of].add(-moved).at[sink].add(moved)
    members = jnp.searchsorted(jnp.cumsum(sizes), jnp.arange(rows * top), side="right").astype(jnp.int32)
    listing = members.reshape(top, rows).T
    listing = listing[jax.random.permutation(jax.random.fold_in(own, 1), rows)]
    turn = jax.random.randint(jax.random.fold_in(own, 2), (rows, 1), 0, top)
    return jnp.take_along_axis(listing, (jnp.arange(top)[None, :] + turn) % top, axis=1)


def load_shares(amount, total, most, slope, full):
    weights = [(1 << 20) // math.isqrt(grade ** slope) + 1 for grade in range(1, amount + 1)]
    largest = most if full else min(most, max(-(-total // amount), total * weights[0] // sum(weights)))
    least = 1 if total - largest >= amount - 1 else 0
    counts, spare = [largest] + [least] * (amount - 1), total - largest - least * (amount - 1)
    while spare > 0:
        movable = [i for i in range(1, amount) if counts[i] < largest] or [i for i in range(1, amount) if counts[i] < most]
        whole, left = sum([weights[i] for i in movable]), spare
        for i in movable:
            more = min(most - counts[i], max(1, left * weights[i] // whole), spare)
            counts[i] = counts[i] + more
            spare = spare - more
    return np.array(counts)


def gaussian(rng, shape, scale, limit, shards=(), kind=jnp.bfloat16):
    factor_of = steps_of(rng, shape, shards, -0.22, 0.18) if shards else 1.0
    drawn = jax.random.normal(rng, shape, jnp.float32) * scale * factor_of
    return jnp.minimum(jnp.maximum(drawn, -limit), limit).astype(kind)


def setup_inputs(seed: int = 0) -> dict:
    key_of = jax.random.split(jax.random.key(seed), 10)
    tokens = gaussian(key_of[0], (TOKENS, D), 1.0, 6.0, ((0, 256),))
    expert_ids_keys = jax.random.split(jax.random.fold_in(key_of[1], 1), TOKENS // TOK_DEV)
    expert_ids_turns = jax.random.permutation(jax.random.fold_in(key_of[1], 3), TOKENS // TOK_DEV)
    expert_ids = jax.vmap(lambda own, number: deal_out(jax.random.fold_in(key_of[1], 2), own, number, TOK_DEV, EXPERTS, TOP, CAP, 2))(expert_ids_keys, expert_ids_turns).reshape((TOKENS, TOP))
    gate_values = jnp.clip(jnp.exp(math.log(1.0) - 2.9957323 * jax.random.uniform(key_of[2], (TOKENS, TOP), jnp.float32) ** steps_of(key_of[2], (TOKENS, TOP), ((0, 256),), -0.2, 0.2)), 0.05, 1.0)
    w_gate = gaussian(key_of[3], (EXPERTS, D, FF), D ** -0.5, 0.09375, ((0, 32), (2, 8)))
    w_up = gaussian(key_of[4], (EXPERTS, D, FF), D ** -0.5, 0.09375, ((0, 32), (2, 8)))
    w_down = gaussian(key_of[5], (EXPERTS, FF, D), FF ** -0.5, 0.125, ((0, 32), (1, 8)))
    s_gate = gaussian(key_of[6], (D, SFF), D ** -0.5, 0.09375, ((1, 8),))
    s_up = gaussian(key_of[7], (D, SFF), D ** -0.5, 0.09375, ((1, 8),))
    s_down = gaussian(key_of[8], (SFF, D), SFF ** -0.5, 0.125, ((0, 8),))
    return {"tokens": tokens, "expert_ids": expert_ids, "gate_values": gate_values, "w_gate": w_gate, "w_up": w_up, "w_down": w_down, "s_gate": s_gate, "s_up": s_up, "s_down": s_down}


def swiglu(rows, gate_w, up_w, down_w):
    gate = jnp.dot(rows, gate_w, preferred_element_type=jnp.float32)
    up = jnp.dot(rows, up_w, preferred_element_type=jnp.float32)
    hidden = (jax.nn.silu(gate) * up).astype(jnp.bfloat16)
    return jnp.dot(hidden, down_w, preferred_element_type=jnp.float32)


def expert_block_sum(rows, gate_w, up_w, down_w):
    gate = jnp.dot(rows, gate_w, preferred_element_type=jnp.float32)
    up = jnp.dot(rows, up_w, preferred_element_type=jnp.float32)
    hidden = (jax.nn.silu(gate) * up).astype(jnp.bfloat16)
    share = FF // N_DP
    blocks = hidden.reshape(rows.shape[0], N_DP, share).astype(jnp.float32)
    downs = down_w.reshape(N_DP, share, D).astype(jnp.float32)
    total = jnp.zeros((rows.shape[0], D), jnp.float32)
    for block in range(N_DP):
        part = jnp.dot(blocks[:, block, :], downs[block], precision=lax.Precision.HIGHEST, preferred_element_type=jnp.float32)
        rounded = lax.optimization_barrier(part.astype(jnp.bfloat16))
        total = total + rounded.astype(jnp.float32)
    return total


def reference(tokens, expert_ids, gate_values, w_gate, w_up, w_down, s_gate, s_up, s_down):
    total = swiglu(tokens, s_gate, s_up, s_down)
    bound = (TOKENS // TOK_DEV) * CAP

    def one_expert(carry, index):
        hits = expert_ids == index
        weight = jnp.sum(jnp.where(hits, gate_values, jnp.float32(0.0)), axis=1)
        chosen = jnp.any(hits, axis=1)
        count = jnp.sum(chosen.astype(jnp.int32)).astype(jnp.int32)
        picked = jnp.nonzero(chosen, size=bound, fill_value=0)[0].astype(jnp.int32)
        outputs = expert_block_sum(tokens[picked], w_gate[index], w_up[index], w_down[index])
        live = jnp.arange(bound, dtype=jnp.int32) < count
        scale = jnp.where(live, weight[picked], jnp.float32(0.0))
        return carry.at[picked].add(scale[:, None] * outputs), None

    indices = jnp.arange(EXPERTS, dtype=jnp.int32)
    total, unused = lax.scan(one_expert, total, indices)
    return total.astype(jnp.bfloat16)
```

```python
import jax
import jax.numpy as jnp
from jax import lax
from jax.experimental import pallas as pl
from jax.experimental.pallas import tpu as pltpu
from jax.sharding import Mesh, PartitionSpec as P

CAP = 3
LANES = 128
SMEM = pltpu.SMEM
VMEM = pltpu.VMEM


def pack_rows(ids, rows3, experts):
    count, picks = ids.shape

    def kernel(ids_ref, rows_ref, out_ref, pos_ref, used_ref):
        out_ref[...] = jnp.zeros_like(out_ref)
        for e in range(experts):
            used_ref[e] = 0
        for r in range(count):
            row = rows_ref[r]
            for k in range(picks):
                e = ids_ref[r, k]
                n = used_ref[e]
                used_ref[e] = n + 1
                slot = e * CAP + n
                pos_ref[r, k] = slot
                out_ref[slot] = row

    return pl.pallas_call(
        kernel,
        out_shape=(
            jax.ShapeDtypeStruct((experts * CAP,) + rows3.shape[1:], rows3.dtype),
            jax.ShapeDtypeStruct(ids.shape, jnp.int32),
        ),
        in_specs=[pl.BlockSpec(memory_space=SMEM), pl.BlockSpec(memory_space=VMEM)],
        out_specs=(pl.BlockSpec(memory_space=VMEM), pl.BlockSpec(memory_space=SMEM)),
        scratch_shapes=[SMEM((experts,), jnp.int32)],
        name="pack_rows",
    )(ids, rows3)


def combine_rows(pos, gates, returned, shared3):
    count, picks = pos.shape

    def kernel(pos_ref, gates_ref, ret_ref, shared_ref, out_ref):
        for r in range(count):
            total = shared_ref[r]
            for k in range(picks):
                total = total + gates_ref[r, k] * ret_ref[pos_ref[r, k]].astype(jnp.float32)
            out_ref[r] = total.astype(out_ref.dtype)

    return pl.pallas_call(
        kernel,
        out_shape=jax.ShapeDtypeStruct(shared3.shape, jnp.bfloat16),
        in_specs=[
            pl.BlockSpec(memory_space=SMEM),
            pl.BlockSpec(memory_space=SMEM),
            pl.BlockSpec(memory_space=VMEM),
            pl.BlockSpec(memory_space=VMEM),
        ],
        out_specs=pl.BlockSpec(memory_space=VMEM),
        name="combine_rows",
    )(pos, gates, returned, shared3)


def hidden_of(rows, gate_w, up_w):
    gate = jnp.dot(rows, gate_w, preferred_element_type=jnp.float32)
    up = jnp.dot(rows, up_w, preferred_element_type=jnp.float32)
    return lax.optimization_barrier((jax.nn.silu(gate) * up).astype(jnp.bfloat16))


def shift(value, axis, by):
    n = lax.axis_size(axis)
    return lax.ppermute(value, axis, [(i, (i + by) % n) for i in range(n)])


def per_device(tokens, ids, gates, w_gate, w_up, w_down, s_gate, s_up, s_down):
    w_gate, w_up, w_down = w_gate[0], w_up[0], w_down[0]
    experts = lax.axis_size(("x", "z"))
    planes = lax.axis_size("y")
    own, width = tokens.shape
    folds = width // LANES
    slots = experts * CAP

    packed, pos = pack_rows(ids, tokens.reshape(own, folds, LANES), experts)
    arrived = lax.all_to_all(
        packed.reshape(experts, CAP, folds, LANES), ("x", "z"), split_axis=0, concat_axis=0, tiled=True
    )
    mine = jnp.concatenate([arrived.reshape(slots, width), tokens], axis=0)

    def ffn(rows):
        routed = jnp.dot(hidden_of(rows[:slots], w_gate, w_up), w_down, preferred_element_type=jnp.float32)
        shared = jnp.dot(hidden_of(rows[slots:], s_gate, s_up), s_down, preferred_element_type=jnp.float32)
        return jnp.concatenate([routed, shared], axis=0)

    blocks = [mine] + [shift(mine, "y", by) for by in range(1, planes)]
    total = None
    for by, block in enumerate(blocks):
        other = shift(block, "core", 1)
        back = shift(ffn(other).astype(jnp.bfloat16), "core", 1)
        both = ffn(block) + back.astype(jnp.float32)
        if by:
            both = shift(both.astype(jnp.bfloat16), "y", planes - by).astype(jnp.float32)
        total = both if total is None else total + both

    routed = total[:slots].astype(jnp.bfloat16).reshape(experts, CAP, folds, LANES)
    returned = lax.all_to_all(routed, ("x", "z"), split_axis=0, concat_axis=0, tiled=True)
    mixed = combine_rows(
        pos, gates, returned.reshape(slots, folds, LANES), total[slots:].reshape(own, folds, LANES)
    )
    return mixed.reshape(own, width)


def solution(mesh):
    fine = Mesh(mesh.devices.reshape(4, 2, 4, 8), ("y", "core", "x", "z"))
    dp, expert = ("y", "core"), ("x", "z")
    placed = (
        P(dp + expert, None),
        P(dp + expert, None),
        P(dp + expert, None),
        P(expert, None, dp),
        P(expert, None, dp),
        P(expert, dp, None),
        P(None, dp),
        P(None, dp),
        P(dp, None),
    )
    return jax.shard_map(
        per_device, mesh=fine, in_specs=placed, out_specs=P(dp + expert, None), check_vma=False
    )
```

```python
import jax
import jax.numpy as jnp
from jax import lax
from jax.experimental import pallas as pl
from jax.experimental.pallas import tpu as pltpu
from jax.sharding import Mesh, PartitionSpec as P

CAP = 3
CHUNKS = ((0, 3),)
LANES = 128
SMALL = pltpu.CompilerParams(vmem_limit_bytes=6 * 2**20)


def in_smem():
    return pl.BlockSpec(memory_space=pltpu.SMEM)


def in_vmem():
    return pl.BlockSpec(memory_space=pltpu.VMEM)


def pack_rows(ids, rows3, experts):
    count, picks = ids.shape

    def kernel(ids_ref, rows_ref, *refs):
        outs, nth_ref, used_ref = refs[: len(CHUNKS)], refs[-2], refs[-1]
        for out_ref in outs:
            out_ref[...] = jnp.zeros_like(out_ref)
        for e in range(experts):
            used_ref[e] = 0
        for r in range(count):
            row = rows_ref[r]
            for k in range(picks):
                e = ids_ref[r, k]
                n = used_ref[e]
                used_ref[e] = n + 1
                nth_ref[r, k] = n
                for (first, end), out_ref in zip(CHUNKS, outs):
                    if len(CHUNKS) == 1:
                        out_ref[e * CAP + n] = row
                    else:

                        @pl.when((n >= first) & (n < end))
                        def _(first=first, end=end, out_ref=out_ref, e=e, n=n, row=row):
                            out_ref[e * (end - first) + (n - first)] = row

    shapes = [
        jax.ShapeDtypeStruct((experts * (end - first),) + rows3.shape[1:], rows3.dtype)
        for first, end in CHUNKS
    ]
    return pl.pallas_call(
        kernel,
        out_shape=(*shapes, jax.ShapeDtypeStruct(ids.shape, jnp.int32)),
        in_specs=[in_smem(), in_vmem()],
        out_specs=(*[in_vmem() for _ in CHUNKS], in_smem()),
        scratch_shapes=[pltpu.SMEM((experts,), jnp.int32)],
        compiler_params=SMALL,
        name="pack_rows",
    )(ids, rows3)


def combine_rows(ids, nth, gates, shared3, *returned):
    count, picks = ids.shape
    ((first, end),) = CHUNKS

    def kernel(ids_ref, nth_ref, gates_ref, shared_ref, ret_ref, out_ref):
        for r in range(count):
            total = shared_ref[r]
            for k in range(picks):
                slot = ids_ref[r, k] * CAP + nth_ref[r, k]
                total = total + gates_ref[r, k] * ret_ref[slot].astype(jnp.float32)
            out_ref[r] = total.astype(out_ref.dtype)

    return pl.pallas_call(
        kernel,
        out_shape=jax.ShapeDtypeStruct(shared3.shape, jnp.bfloat16),
        in_specs=[in_smem(), in_smem(), in_smem(), in_vmem(), in_vmem()],
        out_specs=in_vmem(),
        compiler_params=SMALL,
        name="combine_rows",
    )(ids, nth, gates, shared3, *returned)


def swiglu(rows, *weights):
    total = None
    for gate_w, up_w, down_w in weights:
        gate = jnp.dot(rows, gate_w, preferred_element_type=jnp.float32)
        up = jnp.dot(rows, up_w, preferred_element_type=jnp.float32)
        hidden = lax.optimization_barrier((jax.nn.silu(gate) * up).astype(jnp.bfloat16))
        part = jnp.dot(hidden, down_w, preferred_element_type=jnp.float32)
        total = part if total is None else total + part
    return total


def shift(value, axis, by):
    n = lax.axis_size(axis)
    return lax.ppermute(value, axis, [(i, (i + by) % n) for i in range(n)])


def per_device(tokens, ids, gates, w_gate, w_up, w_down, s_gate, s_up, s_down):
    experts = lax.axis_size(("x", "z"))
    planes = lax.axis_size("y")
    own, width = tokens.shape
    folds = width // LANES

    *packed, nth = pack_rows(ids, tokens.reshape(own, folds, LANES), experts)

    routed_w = (w_gate[0], w_up[0], w_down[0])
    shared_w = (s_gate, s_up, s_down)
    routed_w = (routed_w, tuple(shift(w, "core", 1) for w in routed_w))

    column = jnp.concatenate([tokens] + [shift(tokens, "y", by) for by in range(1, planes)], axis=0)
    column = jnp.concatenate([column, shift(column, "core", 1)], axis=0)
    shared_part = swiglu(column, shared_w)
    rows = planes * own
    shared_part = shared_part[:rows] + shift(shared_part[rows:].astype(jnp.bfloat16), "core", 1).astype(jnp.float32)
    shared_part = shared_part.reshape(planes, own, width)
    shared = shared_part[0]
    for by in range(1, planes):
        shared = shared + shift(shared_part[by].astype(jnp.bfloat16), "y", planes - by).astype(jnp.float32)

    returned = []
    for (first, end), sent in zip(CHUNKS, packed):
        slots = experts * (end - first)
        split = (experts, end - first, folds, LANES)
        arrived = lax.all_to_all(sent.reshape(split), ("x", "z"), split_axis=0, concat_axis=0, tiled=True)
        mine = arrived.reshape(slots, width)
        blocks = [mine] + [shift(mine, "y", by) for by in range(1, planes)]
        total = None
        for by, block in enumerate(blocks):
            part = swiglu(block, *routed_w)
            if by:
                part = shift(part.astype(jnp.bfloat16), "y", planes - by).astype(jnp.float32)
            total = part if total is None else total + part
        back = lax.all_to_all(
            total.astype(jnp.bfloat16).reshape(split), ("x", "z"), split_axis=0, concat_axis=0, tiled=True
        )
        returned.append(back.reshape(slots, folds, LANES))

    mixed = combine_rows(ids, nth, gates, shared.reshape(own, folds, LANES), *returned)
    return mixed.reshape(own, width)


def solution(mesh):
    fine = Mesh(mesh.devices.reshape(4, 2, 4, 8), ("y", "core", "x", "z"))
    dp, expert = ("y", "core"), ("x", "z")
    placed = (
        P(dp + expert, None),
        P(dp + expert, None),
        P(dp + expert, None),
        P(expert, None, dp),
        P(expert, None, dp),
        P(expert, dp, None),
        P(None, dp),
        P(None, dp),
        P(dp, None),
    )
    return jax.shard_map(
        per_device, mesh=fine, in_specs=placed, out_specs=P(dp + expert, None), check_vma=False
    )
```

```python
import jax
import jax.numpy as jnp
from jax import lax
from jax.experimental import pallas as pl
from jax.experimental.pallas import tpu as pltpu
from jax.sharding import Mesh, PartitionSpec as P

CAP = 3
CHUNKS = ((0, 2), (2, 3))
LANES = 128
SMALL = pltpu.CompilerParams(vmem_limit_bytes=6 * 2**20)


def in_smem():
    return pl.BlockSpec(memory_space=pltpu.SMEM)


def in_vmem():
    return pl.BlockSpec(memory_space=pltpu.VMEM)


def pack_rows(ids, rows3, experts):
    count, picks = ids.shape

    def kernel(ids_ref, rows_ref, *refs):
        outs, nth_ref, used_ref = refs[: len(CHUNKS)], refs[-2], refs[-1]
        for out_ref in outs:
            out_ref[...] = jnp.zeros_like(out_ref)
        for e in range(experts):
            used_ref[e] = 0
        for r in range(count):
            row = rows_ref[r]
            for k in range(picks):
                e = ids_ref[r, k]
                n = used_ref[e]
                used_ref[e] = n + 1
                nth_ref[r, k] = n
                for (first, end), out_ref in zip(CHUNKS, outs):
                    if len(CHUNKS) == 1:
                        out_ref[e * CAP + n] = row
                    else:

                        @pl.when((n >= first) & (n < end))
                        def _(first=first, end=end, out_ref=out_ref, e=e, n=n, row=row):
                            out_ref[e * (end - first) + (n - first)] = row

    shapes = [
        jax.ShapeDtypeStruct((experts * (end - first),) + rows3.shape[1:], rows3.dtype)
        for first, end in CHUNKS
    ]
    return pl.pallas_call(
        kernel,
        out_shape=(*shapes, jax.ShapeDtypeStruct(ids.shape, jnp.int32)),
        in_specs=[in_smem(), in_vmem()],
        out_specs=(*[in_vmem() for _ in CHUNKS], in_smem()),
        scratch_shapes=[pltpu.SMEM((experts,), jnp.int32)],
        compiler_params=SMALL,
        name="pack_rows",
    )(ids, rows3)


def combine_rows(ids, nth, gates, start3, returned, chunk, dtype):
    count, picks = ids.shape
    first, end = chunk

    def kernel(ids_ref, nth_ref, gates_ref, start_ref, ret_ref, out_ref):
        for r in range(count):
            total = start_ref[r]
            for k in range(picks):
                n = nth_ref[r, k]
                gate = jnp.where((n >= first) & (n < end), gates_ref[r, k], jnp.float32(0.0))
                slot = ids_ref[r, k] * (end - first) + jnp.minimum(jnp.maximum(n - first, 0), end - first - 1)
                total = total + gate * ret_ref[slot].astype(jnp.float32)
            out_ref[r] = total.astype(out_ref.dtype)

    return pl.pallas_call(
        kernel,
        out_shape=jax.ShapeDtypeStruct(start3.shape, dtype),
        in_specs=[in_smem(), in_smem(), in_smem(), in_vmem(), in_vmem()],
        out_specs=in_vmem(),
        compiler_params=SMALL,
        name="combine_rows",
    )(ids, nth, gates, start3, returned)


def swiglu(rows, weights):
    gate_w, up_w, down_w = weights
    gate = jnp.dot(rows, gate_w, preferred_element_type=jnp.float32)
    up = jnp.dot(rows, up_w, preferred_element_type=jnp.float32)
    hidden = lax.optimization_barrier((jax.nn.silu(gate) * up).astype(jnp.bfloat16))
    return jnp.dot(hidden, down_w, preferred_element_type=jnp.float32)


def shift(value, axis, by):
    n = lax.axis_size(axis)
    return lax.ppermute(value, axis, [(i, (i + by) % n) for i in range(n)])


def layer(tokens, ids, gates, w_gate, w_up, w_down, s_gate, s_up, s_down):
    experts = lax.axis_size(("x", "z"))
    planes = lax.axis_size("y")
    own, width = tokens.shape
    folds = width // LANES

    def exchange(rows, chunk):
        split = (experts, chunk[1] - chunk[0], folds, LANES)
        return lax.all_to_all(rows.reshape(split), ("x", "z"), split_axis=0, concat_axis=0, tiled=True)

    *packed, nth = pack_rows(ids, tokens.reshape(own, folds, LANES), experts)
    early, packed[0] = lax.optimization_barrier((tokens, packed[0]))

    own_w = (w_gate[0], w_up[0], w_down[0])
    other_w = [shift(w, "core", 1) for w in own_w]
    weights = [jnp.concatenate(pair, axis=axis) for pair, axis in zip(zip(own_w, other_w), (1, 1, 0))]

    arrived = exchange(packed[0], CHUNKS[0])

    column = jnp.concatenate([early] + [shift(early, "y", by) for by in range(1, planes)], axis=0)
    column = jnp.concatenate([column, shift(column, "core", 1)], axis=0)
    shared_part = swiglu(column, (s_gate, s_up, s_down))
    rows = planes * own
    shared_part = shared_part[:rows] + shift(shared_part[rows:].astype(jnp.bfloat16), "core", 1).astype(
        jnp.float32
    )
    shared_part = shared_part.reshape(planes, own, width)
    shared = shared_part[0]
    for by in range(1, planes):
        back = shift(shared_part[by].astype(jnp.bfloat16), "y", planes - by)
        shared = shared + back.astype(jnp.float32)

    arrived, *weights = lax.optimization_barrier((arrived, *weights))
    arrived = [arrived]
    for index in range(1, len(CHUNKS)):
        sent, arrived[-1] = lax.optimization_barrier((packed[index], arrived[-1]))
        arrived.append(exchange(sent, CHUNKS[index]))

    mixed = shared.reshape(own, folds, LANES)
    for chunk, rows3 in zip(CHUNKS, arrived):
        slots = experts * (chunk[1] - chunk[0])
        mine = rows3.reshape(slots, width)
        near = [shift(mine, "y", by) for by in (1, planes - 1)]
        later, *near = lax.optimization_barrier((mine, *near))
        far = shift(later, "y", 2)
        total = swiglu(mine, weights)
        part = swiglu(jnp.concatenate(near, axis=0), weights).astype(jnp.bfloat16)
        back = [shift(part[:slots], "y", planes - 1), shift(part[slots:], "y", 1)]
        part = swiglu(far, weights).astype(jnp.bfloat16)
        back.append(shift(part, "y", 2))
        for part in back:
            total = total + part.astype(jnp.float32)
        returned = exchange(total.astype(jnp.bfloat16), chunk).reshape(slots, folds, LANES)
        mixed = combine_rows(
            ids, nth, gates, mixed, returned, chunk, jnp.bfloat16 if chunk == CHUNKS[-1] else jnp.float32
        )
    return mixed.reshape(own, width)


def solution(mesh):
    fine = Mesh(mesh.devices.reshape(4, 2, 4, 8), ("y", "core", "x", "z"))
    dp, expert = ("y", "core"), ("x", "z")
    placed = (
        P(dp + expert, None),
        P(dp + expert, None),
        P(dp + expert, None),
        P(expert, None, dp),
        P(expert, None, dp),
        P(expert, dp, None),
        P(None, dp),
        P(None, dp),
        P(dp, None),
    )
    return jax.shard_map(layer, mesh=fine, in_specs=placed, out_specs=P(dp + expert, None), check_vma=False)
```

```python
import jax
import jax.numpy as jnp
from jax import lax
from jax.experimental import pallas as pl
from jax.experimental.pallas import tpu as pltpu
from jax.sharding import Mesh, PartitionSpec as P

CAP = 3
PARTS = 1
LANES = 128
SMALL = pltpu.CompilerParams(vmem_limit_bytes=6 * 2**20)


def in_smem():
    return pl.BlockSpec(memory_space=pltpu.SMEM)


def in_vmem():
    return pl.BlockSpec(memory_space=pltpu.VMEM)


def pack_rows(ids, rows3, experts):
    count, picks = ids.shape

    def kernel(ids_ref, rows_ref, out_ref, slot_ref, used_ref):
        out_ref[...] = jnp.zeros_like(out_ref)
        for e in range(experts):
            used_ref[e] = 0
        for r in range(count):
            row = rows_ref[r]
            for k in range(picks):
                e = ids_ref[r, k]
                n = used_ref[e]
                used_ref[e] = n + 1
                slot = e * CAP + n
                slot_ref[r, k] = slot
                out_ref[slot] = row

    return pl.pallas_call(
        kernel,
        out_shape=(
            jax.ShapeDtypeStruct((experts * CAP,) + rows3.shape[1:], rows3.dtype),
            jax.ShapeDtypeStruct(ids.shape, jnp.int32),
        ),
        in_specs=[in_smem(), in_vmem()],
        out_specs=(in_vmem(), in_smem()),
        scratch_shapes=[pltpu.SMEM((experts,), jnp.int32)],
        compiler_params=SMALL,
        name="pack_rows",
    )(ids, rows3)


def combine_rows(slots, gates, shared3, *returned):
    count, picks = slots.shape
    folds = shared3.shape[1] // len(returned)

    def kernel(slot_ref, gates_ref, shared_ref, *refs):
        out_ref = refs[-1]
        for index, ret_ref in enumerate(refs[:-1]):
            part = slice(index * folds, (index + 1) * folds)
            for r in range(count):
                total = shared_ref[r, part]
                for k in range(picks):
                    total = total + gates_ref[r, k] * ret_ref[slot_ref[r, k]].astype(jnp.float32)
                out_ref[r, part] = total.astype(out_ref.dtype)

    return pl.pallas_call(
        kernel,
        out_shape=jax.ShapeDtypeStruct(shared3.shape, jnp.bfloat16),
        in_specs=[in_smem(), in_smem(), in_vmem()] + [in_vmem() for _ in returned],
        out_specs=in_vmem(),
        compiler_params=SMALL,
        name="combine_rows",
    )(slots, gates, shared3, *returned)


def hidden_of(rows, gate_w, up_w):
    gate = jnp.dot(rows, gate_w, preferred_element_type=jnp.float32)
    up = jnp.dot(rows, up_w, preferred_element_type=jnp.float32)
    return lax.optimization_barrier((jax.nn.silu(gate) * up).astype(jnp.bfloat16))


def down(hidden, down_w):
    return jnp.dot(hidden, down_w, preferred_element_type=jnp.float32)


def shift(value, axis, by):
    n = lax.axis_size(axis)
    return lax.ppermute(value, axis, [(i, (i + by) % n) for i in range(n)])


def layer(tokens, ids, gates, w_gate, w_up, w_down, s_gate, s_up, s_down):
    experts = lax.axis_size(("x", "z"))
    planes = lax.axis_size("y")
    own, width = tokens.shape
    folds = width // LANES
    slots = experts * CAP
    half = slots // 2

    def exchange(rows, part):
        split = (experts, CAP, part, LANES)
        arrived = lax.all_to_all(rows.reshape(split), ("x", "z"), split_axis=0, concat_axis=0, tiled=True)
        return arrived.reshape(slots, part, LANES)

    packed, places = pack_rows(ids, tokens.reshape(own, folds, LANES), experts)
    early, packed = lax.optimization_barrier((tokens, packed))

    own_w = (w_gate[0], w_up[0], w_down[0])
    other_w = [shift(w, "core", 1) for w in own_w]
    gate_w, up_w = (jnp.concatenate(pair, axis=1) for pair in zip(own_w[:2], other_w[:2]))
    step = width // PARTS
    down_w = [
        jnp.concatenate([w[:, part * step : (part + 1) * step] for w in (own_w[2], other_w[2])], axis=0)
        for part in range(PARTS)
    ]

    arrived = exchange(packed, folds)

    column = jnp.concatenate([early] + [shift(early, "y", by) for by in range(1, planes)], axis=0)
    column = jnp.concatenate([column, shift(column, "core", 1)], axis=0)
    shared_part = down(hidden_of(column, s_gate, s_up), s_down)
    rows = planes * own
    back = shift(shared_part[rows:].astype(jnp.bfloat16), "core", 1)
    shared_part = (shared_part[:rows] + back.astype(jnp.float32)).reshape(planes, own, width)
    shared = shared_part[0]
    for by in range(1, planes):
        back = shift(shared_part[by].astype(jnp.bfloat16), "y", planes - by)
        shared = shared + back.astype(jnp.float32)

    gate_w, up_w, *down_w = lax.optimization_barrier((gate_w, up_w, *down_w))

    mine = arrived.reshape(slots, width)
    left, right = shift(mine, "y", 1), shift(mine, "y", planes - 1)
    far = [shift(left[:half], "y", 1), shift(right[half:], "y", planes - 1)]
    far = jnp.concatenate(far, axis=0)

    own_hidden = hidden_of(mine, gate_w, up_w)
    total = [down(own_hidden, w) for w in down_w]
    near_hidden = hidden_of(jnp.concatenate([left, right], axis=0), gate_w, up_w)
    near = [down(near_hidden, w).astype(jnp.bfloat16) for w in down_w]
    far_hidden = hidden_of(far, gate_w, up_w)
    far = [down(far_hidden, w).astype(jnp.bfloat16) for w in down_w]

    returned = []
    for part in range(PARTS):
        back = [shift(near[part][:slots], "y", planes - 1), shift(near[part][slots:], "y", 1)]
        back.append(shift(far[part], "y", 2))
        for value in back:
            total[part] = total[part] + value.astype(jnp.float32)
        returned.append(exchange(total[part].astype(jnp.bfloat16), folds // PARTS))

    mixed = combine_rows(places, gates, shared.reshape(own, folds, LANES), *returned)
    return mixed.reshape(own, width)


def solution(mesh):
    fine = Mesh(mesh.devices.reshape(4, 2, 4, 8), ("y", "core", "x", "z"))
    dp, expert = ("y", "core"), ("x", "z")
    placed = (
        P(dp + expert, None),
        P(dp + expert, None),
        P(dp + expert, None),
        P(expert, None, dp),
        P(expert, None, dp),
        P(expert, dp, None),
        P(None, dp),
        P(None, dp),
        P(dp, None),
    )
    return jax.shard_map(layer, mesh=fine, in_specs=placed, out_specs=P(dp + expert, None), check_vma=False)
```

```python
import jax
import jax.numpy as jnp
from jax import lax
from jax.experimental import pallas as pl
from jax.experimental.pallas import tpu as pltpu
from jax.sharding import Mesh, PartitionSpec as P

CAP = 3
LANES = 128
SMALL = pltpu.CompilerParams(vmem_limit_bytes=6 * 2**20)


def in_smem():
    return pl.BlockSpec(memory_space=pltpu.SMEM)


def in_vmem():
    return pl.BlockSpec(memory_space=pltpu.VMEM)


def pack_rows(ids, rows3, experts):
    count, picks = ids.shape

    def kernel(ids_ref, rows_ref, out_ref, slot_ref, used_ref):
        out_ref[...] = jnp.zeros_like(out_ref)
        for e in range(experts):
            used_ref[e] = 0
        for r in range(count):
            row = rows_ref[r]
            for k in range(picks):
                e = ids_ref[r, k]
                n = used_ref[e]
                used_ref[e] = n + 1
                slot = e * CAP + n
                slot_ref[r, k] = slot
                out_ref[slot] = row

    return pl.pallas_call(
        kernel,
        out_shape=(
            jax.ShapeDtypeStruct((experts * CAP,) + rows3.shape[1:], rows3.dtype),
            jax.ShapeDtypeStruct(ids.shape, jnp.int32),
        ),
        in_specs=[in_smem(), in_vmem()],
        out_specs=(in_vmem(), in_smem()),
        scratch_shapes=[pltpu.SMEM((experts,), jnp.int32)],
        compiler_params=SMALL,
        name="pack_rows",
    )(ids, rows3)


def combine_rows(slots, gates, shared3, returned):
    count, picks = slots.shape

    def kernel(slot_ref, gates_ref, shared_ref, ret_ref, out_ref):
        for r in range(count):
            total = shared_ref[r]
            for k in range(picks):
                total = total + gates_ref[r, k] * ret_ref[slot_ref[r, k]].astype(jnp.float32)
            out_ref[r] = total.astype(out_ref.dtype)

    return pl.pallas_call(
        kernel,
        out_shape=jax.ShapeDtypeStruct(shared3.shape, jnp.bfloat16),
        in_specs=[in_smem(), in_smem(), in_vmem(), in_vmem()],
        out_specs=in_vmem(),
        compiler_params=SMALL,
        name="combine_rows",
    )(slots, gates, shared3, returned)


def hidden_of(rows, gate_w, up_w):
    gate = jnp.dot(rows, gate_w, preferred_element_type=jnp.float32)
    up = jnp.dot(rows, up_w, preferred_element_type=jnp.float32)
    return lax.optimization_barrier((jax.nn.silu(gate) * up).astype(jnp.bfloat16))


def down(hidden, down_w):
    return jnp.dot(hidden, down_w, preferred_element_type=jnp.float32)


def shift(value, axis, by):
    n = lax.axis_size(axis)
    return lax.ppermute(value, axis, [(i, (i + by) % n) for i in range(n)])


def layer(tokens, ids, gates, w_gate, w_up, w_down, s_gate, s_up, s_down):
    experts = lax.axis_size(("x", "z"))
    planes = lax.axis_size("y")
    own, width = tokens.shape
    folds = width // LANES
    slots = experts * CAP
    half = slots // 2

    def exchange(rows, part):
        split = (experts, CAP, part, LANES)
        arrived = lax.all_to_all(rows.reshape(split), ("x", "z"), split_axis=0, concat_axis=0, tiled=True)
        return arrived.reshape(slots, part, LANES)

    packed, places = pack_rows(ids, tokens.reshape(own, folds, LANES), experts)
    early, packed = lax.optimization_barrier((tokens, packed))

    own_w = (w_gate[0], w_up[0], w_down[0])
    other_w = [shift(w, "core", 1) for w in own_w]
    gate_w, up_w = (jnp.concatenate(pair, axis=1) for pair in zip(own_w[:2], other_w[:2]))
    down_w = jnp.concatenate([own_w[2], other_w[2]], axis=0)

    arrived = exchange(packed, folds)

    column = jnp.concatenate([early] + [shift(early, "y", by) for by in range(1, planes)], axis=0)
    column = jnp.concatenate([column, shift(column, "core", 1)], axis=0)
    shared_part = down(hidden_of(column, s_gate, s_up), s_down)
    rows = planes * own
    back = shift(shared_part[rows:].astype(jnp.bfloat16), "core", 1)
    shared_part = (shared_part[:rows] + back.astype(jnp.float32)).reshape(planes, own, width)
    shared = shared_part[0]
    for by in range(1, planes):
        back = shift(shared_part[by].astype(jnp.bfloat16), "y", planes - by)
        shared = shared + back.astype(jnp.float32)

    gate_w, up_w, down_w = lax.optimization_barrier((gate_w, up_w, down_w))

    mine = arrived.reshape(slots, width)
    left, right = shift(mine, "y", 1), shift(mine, "y", planes - 1)
    far = [shift(left[:half], "y", 1), shift(right[half:], "y", planes - 1)]
    far = jnp.concatenate(far, axis=0)

    total = down(hidden_of(mine, gate_w, up_w), down_w)
    near = hidden_of(jnp.concatenate([left[:half], right[half:], left[half:], right[:half]], axis=0), gate_w, up_w)
    free = down(near[:slots], down_w).astype(jnp.bfloat16)
    held = down(near[slots:], down_w)
    free = shift(free[half:], "y", 1), shift(free[:half], "y", planes - 1)
    far = down(hidden_of(far, gate_w, up_w), down_w).astype(jnp.bfloat16)
    far = shift(far[:half], "y", 1), shift(far[half:], "y", planes - 1)
    upper = (held[half:] + far[0].astype(jnp.float32)).astype(jnp.bfloat16)
    lower = (held[:half] + far[1].astype(jnp.float32)).astype(jnp.bfloat16)
    held = shift(upper, "y", 1), shift(lower, "y", planes - 1)
    back = (held[0], free[1]), (free[0], held[1])
    back = [sum(value.astype(jnp.float32) for value in values) for values in back]
    total = total + jnp.concatenate(back, axis=0)
    returned = exchange(total.astype(jnp.bfloat16), folds)

    mixed = combine_rows(places, gates, shared.reshape(own, folds, LANES), returned)
    return mixed.reshape(own, width)


def solution(mesh):
    fine = Mesh(mesh.devices.reshape(4, 2, 4, 8), ("y", "core", "x", "z"))
    dp, expert = ("y", "core"), ("x", "z")
    placed = (
        P(dp + expert, None),
        P(dp + expert, None),
        P(dp + expert, None),
        P(expert, None, dp),
        P(expert, None, dp),
        P(expert, dp, None),
        P(None, dp),
        P(None, dp),
        P(dp, None),
    )
    return jax.shard_map(layer, mesh=fine, in_specs=placed, out_specs=P(dp + expert, None), check_vma=False)
```

```python
import jax
import jax.numpy as jnp
from jax import lax
from jax.experimental import pallas as pl
from jax.experimental.pallas import tpu as pltpu
from jax.sharding import Mesh, PartitionSpec as P

CAP = 3
LANES = 128
SMALL = pltpu.CompilerParams(vmem_limit_bytes=6 * 2**20)


def in_smem():
    return pl.BlockSpec(memory_space=pltpu.SMEM)


def in_vmem():
    return pl.BlockSpec(memory_space=pltpu.VMEM)


def pack_rows(ids, rows3, experts, order):
    count, picks = ids.shape

    def kernel(ids_ref, rows_ref, out_ref, slot_ref, used_ref):
        out_ref[...] = jnp.zeros_like(out_ref)
        for e in range(experts):
            used_ref[e] = 0
        for r in range(count):
            row = rows_ref[r]
            for k in range(picks):
                e = ids_ref[r, k]
                n = used_ref[e]
                used_ref[e] = n + 1
                slot = order(e) * CAP + n
                slot_ref[r, k] = slot
                out_ref[slot] = row

    return pl.pallas_call(
        kernel,
        out_shape=(
            jax.ShapeDtypeStruct((experts * CAP,) + rows3.shape[1:], rows3.dtype),
            jax.ShapeDtypeStruct(ids.shape, jnp.int32),
        ),
        in_specs=[in_smem(), in_vmem()],
        out_specs=(in_vmem(), in_smem()),
        scratch_shapes=[pltpu.SMEM((experts,), jnp.int32)],
        compiler_params=SMALL,
        name="pack_rows",
    )(ids, rows3)


def combine_rows(slots, gates, shared3, returned):
    count, picks = slots.shape

    def kernel(slot_ref, gates_ref, shared_ref, ret_ref, out_ref):
        for r in range(count):
            total = shared_ref[r]
            for k in range(picks):
                total = total + gates_ref[r, k] * ret_ref[slot_ref[r, k]].astype(jnp.float32)
            out_ref[r] = total.astype(out_ref.dtype)

    return pl.pallas_call(
        kernel,
        out_shape=jax.ShapeDtypeStruct(shared3.shape, jnp.bfloat16),
        in_specs=[in_smem(), in_smem(), in_vmem(), in_vmem()],
        out_specs=in_vmem(),
        compiler_params=SMALL,
        name="combine_rows",
    )(slots, gates, shared3, returned)


def hidden_of(rows, gate_w, up_w):
    gate = jnp.dot(rows, gate_w, preferred_element_type=jnp.float32)
    up = jnp.dot(rows, up_w, preferred_element_type=jnp.float32)
    return lax.optimization_barrier((jax.nn.silu(gate) * up).astype(jnp.bfloat16))


def down(hidden, down_w):
    return jnp.dot(hidden, down_w, preferred_element_type=jnp.float32)


def shift(value, axis, by):
    n = lax.axis_size(axis)
    return lax.ppermute(value, axis, [(i, (i + by) % n) for i in range(n)])


def layer(tokens, ids, gates, w_gate, w_up, w_down, s_gate, s_up, s_down):
    experts = lax.axis_size(("x", "z"))
    planes, columns = lax.axis_size("y"), lax.axis_size("x")
    own, width = tokens.shape
    folds = width // LANES
    slots = experts * CAP
    half = slots // 2

    def by_z(e):
        return lax.rem(e, experts // columns) * columns + lax.div(e, experts // columns)

    def exchange(rows, part):
        split = (experts, CAP, part, LANES)
        arrived = lax.all_to_all(rows.reshape(split), ("z", "x"), split_axis=0, concat_axis=0, tiled=True)
        return arrived.reshape(slots, part, LANES)

    packed, places = pack_rows(ids, tokens.reshape(own, folds, LANES), experts, by_z)
    early, packed = lax.optimization_barrier((tokens, packed))

    own_w = (w_gate[0], w_up[0], w_down[0])
    other_w = [shift(w, "core", 1) for w in own_w]
    gate_w, up_w = (jnp.concatenate(pair, axis=1) for pair in zip(own_w[:2], other_w[:2]))
    down_w = jnp.concatenate([own_w[2], other_w[2]], axis=0)

    arrived = exchange(packed, folds)

    column = jnp.concatenate([early] + [shift(early, "y", by) for by in range(1, planes)], axis=0)
    column = jnp.concatenate([column, shift(column, "core", 1)], axis=0)
    shared_part = down(hidden_of(column, s_gate, s_up), s_down)
    rows = planes * own
    back = shift(shared_part[rows:].astype(jnp.bfloat16), "core", 1)
    shared_part = (shared_part[:rows] + back.astype(jnp.float32)).reshape(planes, own, width)
    shared = shared_part[0]
    for by in range(1, planes):
        back = shift(shared_part[by].astype(jnp.bfloat16), "y", planes - by)
        shared = shared + back.astype(jnp.float32)

    gate_w, up_w, down_w = lax.optimization_barrier((gate_w, up_w, down_w))

    mine = arrived.reshape(slots, width)
    left, right = shift(mine, "y", 1), shift(mine, "y", planes - 1)
    far = [shift(left[:half], "y", 1), shift(right[half:], "y", planes - 1)]
    far = jnp.concatenate(far, axis=0)

    total = down(hidden_of(mine, gate_w, up_w), down_w)
    near = hidden_of(jnp.concatenate([left[:half], right[half:], left[half:], right[:half]], axis=0), gate_w, up_w)
    free = down(near[:slots], down_w).astype(jnp.bfloat16)
    held = down(near[slots:], down_w)
    free = shift(free[half:], "y", 1), shift(free[:half], "y", planes - 1)
    far = down(hidden_of(far, gate_w, up_w), down_w).astype(jnp.bfloat16)
    far = shift(far[:half], "y", 1), shift(far[half:], "y", planes - 1)
    upper = (held[half:] + far[0].astype(jnp.float32)).astype(jnp.bfloat16)
    lower = (held[:half] + far[1].astype(jnp.float32)).astype(jnp.bfloat16)
    held = shift(upper, "y", 1), shift(lower, "y", planes - 1)
    back = (held[0], free[1]), (free[0], held[1])
    back = [sum(value.astype(jnp.float32) for value in values) for values in back]
    total = total + jnp.concatenate(back, axis=0)
    returned = exchange(total.astype(jnp.bfloat16), folds)

    mixed = combine_rows(places, gates, shared.reshape(own, folds, LANES), returned)
    return mixed.reshape(own, width)


def solution(mesh):
    fine = Mesh(mesh.devices.reshape(4, 2, 4, 8), ("y", "core", "x", "z"))
    dp, expert = ("y", "core"), ("x", "z")
    placed = (
        P(dp + expert, None),
        P(dp + expert, None),
        P(dp + expert, None),
        P(expert, None, dp),
        P(expert, None, dp),
        P(expert, dp, None),
        P(None, dp),
        P(None, dp),
        P(dp, None),
    )
    return jax.shard_map(layer, mesh=fine, in_specs=placed, out_specs=P(dp + expert, None), check_vma=False)
```

```python
import jax
import jax.numpy as jnp
from jax import lax
from jax.experimental import pallas as pl
from jax.experimental.pallas import tpu as pltpu
from jax.sharding import Mesh, PartitionSpec as P

CAP = 3
LANES = 128
SMALL = pltpu.CompilerParams(vmem_limit_bytes=6 * 2**20)


def in_smem():
    return pl.BlockSpec(memory_space=pltpu.SMEM)


def in_vmem():
    return pl.BlockSpec(memory_space=pltpu.VMEM)


def pack_rows(ids, rows, experts, order):
    count, picks = ids.shape
    folds = rows.shape[1] // LANES

    def kernel(ids_hbm, rows_hbm, out_ref, slot_ref, ids_ref, rows_ref, rows3_ref, used_ref, sems):
        copies = (
            pltpu.make_async_copy(ids_hbm, ids_ref, sems.at[0]),
            pltpu.make_async_copy(rows_hbm, rows_ref, sems.at[1]),
        )
        for copy in copies:
            copy.start()
        out_ref[...] = jnp.zeros_like(out_ref)
        for e in range(experts):
            used_ref[e] = 0
        for copy in copies:
            copy.wait()
        for c in range(folds):
            rows3_ref[:, c, :] = rows_ref[:, c * LANES : (c + 1) * LANES].astype(jnp.float32)
        for r in range(count):
            row = rows3_ref[r].astype(out_ref.dtype)
            for k in range(picks):
                e = ids_ref[r, k]
                n = used_ref[e]
                used_ref[e] = n + 1
                slot = order(e) * CAP + n
                slot_ref[r, k] = slot
                out_ref[slot] = row

    return pl.pallas_call(
        kernel,
        out_shape=(
            jax.ShapeDtypeStruct((experts * CAP, folds, LANES), rows.dtype),
            jax.ShapeDtypeStruct(ids.shape, jnp.int32),
        ),
        in_specs=[pl.BlockSpec(memory_space=pltpu.HBM)] * 2,
        out_specs=(in_vmem(), in_smem()),
        scratch_shapes=[
            pltpu.SMEM(ids.shape, jnp.int32),
            pltpu.VMEM(rows.shape, rows.dtype),
            pltpu.VMEM((count, folds, LANES), jnp.float32),
            pltpu.SMEM((experts,), jnp.int32),
            pltpu.SemaphoreType.DMA((2,)),
        ],
        compiler_params=pltpu.CompilerParams(vmem_limit_bytes=62 * 2**20),
        name="pack_rows",
    )(ids, rows)


def combine_rows(slots, gates, shared, returned):
    count, picks = slots.shape

    folds = returned.shape[1]

    def kernel(slot_ref, gates_ref, shared_ref, ret_ref, out_ref, routed_ref):
        for r in range(count):
            total = gates_ref[r, 0] * ret_ref[slot_ref[r, 0]].astype(jnp.float32)
            for k in range(1, picks):
                total = total + gates_ref[r, k] * ret_ref[slot_ref[r, k]].astype(jnp.float32)
            routed_ref[r] = total
        for c in range(folds):
            part = slice(c * LANES, (c + 1) * LANES)
            out_ref[:, part] = (shared_ref[:, part] + routed_ref[:, c, :]).astype(out_ref.dtype)

    return pl.pallas_call(
        kernel,
        out_shape=jax.ShapeDtypeStruct(shared.shape, jnp.bfloat16),
        in_specs=[in_smem(), in_smem(), in_vmem(), in_vmem()],
        out_specs=in_vmem(),
        scratch_shapes=[pltpu.VMEM((count, folds, LANES), jnp.float32)],
        compiler_params=SMALL,
        name="combine_rows",
    )(slots, gates, shared, returned)


def hidden_of(rows, gate_w, up_w):
    gate = jnp.dot(rows, gate_w, preferred_element_type=jnp.float32)
    up = jnp.dot(rows, up_w, preferred_element_type=jnp.float32)
    return lax.optimization_barrier((jax.nn.silu(gate) * up).astype(jnp.bfloat16))


def down(hidden, down_w):
    return jnp.dot(hidden, down_w, preferred_element_type=jnp.float32)


def shift(value, axis, by):
    n = lax.axis_size(axis)
    return lax.ppermute(value, axis, [(i, (i + by) % n) for i in range(n)])


def layer(tokens, ids, gates, w_gate, w_up, w_down, s_gate, s_up, s_down):
    experts = lax.axis_size(("x", "z"))
    planes, columns = lax.axis_size("y"), lax.axis_size("x")
    own, width = tokens.shape
    folds = width // LANES
    slots = experts * CAP
    half = slots // 2

    def by_z(e):
        return lax.rem(e, experts // columns) * columns + lax.div(e, experts // columns)

    def exchange(rows, part):
        split = (experts, CAP, part, LANES)
        arrived = lax.all_to_all(rows.reshape(split), ("z", "x"), split_axis=0, concat_axis=0, tiled=True)
        return arrived.reshape(slots, part, LANES)

    packed, places = pack_rows(ids, tokens, experts, by_z)
    early, packed = lax.optimization_barrier((tokens, packed))

    own_w = (w_gate[0], w_up[0], w_down[0])
    other_w = [shift(w, "core", 1) for w in own_w]
    gate_w, up_w = (jnp.concatenate(pair, axis=1) for pair in zip(own_w[:2], other_w[:2]))
    down_w = jnp.concatenate([own_w[2], other_w[2]], axis=0)

    arrived = exchange(packed, folds)

    column = jnp.concatenate([early] + [shift(early, "y", by) for by in range(1, planes)], axis=0)
    column = jnp.concatenate([column, shift(column, "core", 1)], axis=0)
    shared_part = down(hidden_of(column, s_gate, s_up), s_down)
    rows = planes * own
    back = shift(shared_part[rows:].astype(jnp.bfloat16), "core", 1)
    shared_part = (shared_part[:rows] + back.astype(jnp.float32)).reshape(planes, own, width)
    shared = shared_part[0]
    for by in range(1, planes):
        back = shift(shared_part[by].astype(jnp.bfloat16), "y", planes - by)
        shared = shared + back.astype(jnp.float32)

    gate_w, up_w, down_w = lax.optimization_barrier((gate_w, up_w, down_w))

    mine = arrived.reshape(slots, width)
    left, right = shift(mine, "y", 1), shift(mine, "y", planes - 1)
    far = [shift(left[:half], "y", 1), shift(right[half:], "y", planes - 1)]
    far = jnp.concatenate(far, axis=0)

    total = down(hidden_of(mine, gate_w, up_w), down_w)
    near = hidden_of(jnp.concatenate([left[:half], right[half:], left[half:], right[:half]], axis=0), gate_w, up_w)
    free = down(near[:slots], down_w).astype(jnp.bfloat16)
    held = down(near[slots:], down_w)
    free = shift(free[half:], "y", 1), shift(free[:half], "y", planes - 1)
    far = down(hidden_of(far, gate_w, up_w), down_w).astype(jnp.bfloat16)
    far = shift(far[:half], "y", 1), shift(far[half:], "y", planes - 1)
    upper = (held[half:] + far[0].astype(jnp.float32)).astype(jnp.bfloat16)
    lower = (held[:half] + far[1].astype(jnp.float32)).astype(jnp.bfloat16)
    held = shift(upper, "y", 1), shift(lower, "y", planes - 1)
    back = (held[0], free[1]), (free[0], held[1])
    back = [sum(value.astype(jnp.float32) for value in values) for values in back]
    total = total + jnp.concatenate(back, axis=0)
    returned = exchange(total.astype(jnp.bfloat16), folds)

    return combine_rows(places, gates, shared, returned)


def solution(mesh):
    fine = Mesh(mesh.devices.reshape(4, 2, 4, 8), ("y", "core", "x", "z"))
    dp, expert = ("y", "core"), ("x", "z")
    placed = (
        P(dp + expert, None),
        P(dp + expert, None),
        P(dp + expert, None),
        P(expert, None, dp),
        P(expert, None, dp),
        P(expert, dp, None),
        P(None, dp),
        P(None, dp),
        P(dp, None),
    )
    return jax.shard_map(layer, mesh=fine, in_specs=placed, out_specs=P(dp + expert, None), check_vma=False)
```

```python
import jax
import jax.numpy as jnp
from jax import lax
from jax.experimental import pallas as pl
from jax.experimental.pallas import tpu as pltpu
from jax.sharding import Mesh, PartitionSpec as P

CAP = 3
LANES = 128
SMALL = pltpu.CompilerParams(vmem_limit_bytes=6 * 2**20)


def in_smem():
    return pl.BlockSpec(memory_space=pltpu.SMEM)


def in_vmem():
    return pl.BlockSpec(memory_space=pltpu.VMEM)


def pack_rows(ids, rows, experts, order):
    count, picks = ids.shape
    folds = rows.shape[1] // LANES

    def kernel(ids_hbm, rows_hbm, out_ref, slot_ref, ids_ref, rows_ref, rows3_ref, used_ref, sems):
        copies = (
            pltpu.make_async_copy(ids_hbm, ids_ref, sems.at[0]),
            pltpu.make_async_copy(rows_hbm, rows_ref, sems.at[1]),
        )
        for copy in copies:
            copy.start()
        out_ref[...] = jnp.zeros_like(out_ref)
        for e in range(experts):
            used_ref[e] = 0
        for copy in copies:
            copy.wait()
        for c in range(folds):
            rows3_ref[:, c, :] = rows_ref[:, c * LANES : (c + 1) * LANES].astype(jnp.float32)
        for r in range(count):
            row = rows3_ref[r].astype(out_ref.dtype)
            for k in range(picks):
                e = ids_ref[r, k]
                n = used_ref[e]
                used_ref[e] = n + 1
                slot = order(e) * CAP + n
                slot_ref[r, k] = slot
                out_ref[slot] = row

    return pl.pallas_call(
        kernel,
        out_shape=(
            jax.ShapeDtypeStruct((experts * CAP, folds, LANES), rows.dtype),
            jax.ShapeDtypeStruct(ids.shape, jnp.int32),
        ),
        in_specs=[pl.BlockSpec(memory_space=pltpu.HBM)] * 2,
        out_specs=(in_vmem(), in_smem()),
        scratch_shapes=[
            pltpu.SMEM(ids.shape, jnp.int32),
            pltpu.VMEM(rows.shape, rows.dtype),
            pltpu.VMEM((count, folds, LANES), jnp.float32),
            pltpu.SMEM((experts,), jnp.int32),
            pltpu.SemaphoreType.DMA((2,)),
        ],
        compiler_params=pltpu.CompilerParams(vmem_limit_bytes=62 * 2**20),
        name="pack_rows",
    )(ids, rows)


def combine_rows(slots, gates, shared, returned):
    count, picks = slots.shape

    folds = returned.shape[1]

    def kernel(slot_ref, gates_ref, shared_ref, ret_ref, out_ref, routed_ref):
        for r in range(count):
            total = gates_ref[r, 0] * ret_ref[slot_ref[r, 0]].astype(jnp.float32)
            for k in range(1, picks):
                total = total + gates_ref[r, k] * ret_ref[slot_ref[r, k]].astype(jnp.float32)
            routed_ref[r] = total
        for c in range(folds):
            part = slice(c * LANES, (c + 1) * LANES)
            out_ref[:, part] = (shared_ref[:, part] + routed_ref[:, c, :]).astype(out_ref.dtype)

    return pl.pallas_call(
        kernel,
        out_shape=jax.ShapeDtypeStruct(shared.shape, jnp.bfloat16),
        in_specs=[in_smem(), in_smem(), in_vmem(), in_vmem()],
        out_specs=in_vmem(),
        scratch_shapes=[pltpu.VMEM((count, folds, LANES), jnp.float32)],
        compiler_params=SMALL,
        name="combine_rows",
    )(slots, gates, shared, returned)


def hidden_of(rows, gate_w, up_w):
    gate = jnp.dot(rows, gate_w, preferred_element_type=jnp.float32)
    up = jnp.dot(rows, up_w, preferred_element_type=jnp.float32)
    return lax.optimization_barrier((jax.nn.silu(gate) * up).astype(jnp.bfloat16))


def down(hidden, down_w):
    return jnp.dot(hidden, down_w, preferred_element_type=jnp.float32)


def shift(value, axis, by):
    n = lax.axis_size(axis)
    return lax.ppermute(value, axis, [(i, (i + by) % n) for i in range(n)])


def layer(tokens, ids, gates, w_gate, w_up, w_down, s_gate, s_up, s_down):
    experts = lax.axis_size(("x", "z"))
    planes, columns = lax.axis_size("y"), lax.axis_size("x")
    own, width = tokens.shape
    folds = width // LANES
    slots = experts * CAP
    half = slots // 2

    def by_z(e):
        return lax.rem(e, experts // columns) * columns + lax.div(e, experts // columns)

    def exchange(rows, part):
        split = (experts, CAP, part, LANES)
        arrived = lax.all_to_all(rows.reshape(split), ("z", "x"), split_axis=0, concat_axis=0, tiled=True)
        return arrived.reshape(slots, part, LANES)

    packed, places = pack_rows(ids, tokens, experts, by_z)
    early, packed = lax.optimization_barrier((tokens, packed))

    own_w = (w_gate[0], w_up[0], w_down[0])
    other_w = [shift(w, "core", 1) for w in own_w]
    gate_w, up_w = (jnp.concatenate(pair, axis=1) for pair in zip(own_w[:2], other_w[:2]))
    down_w = jnp.concatenate([own_w[2], other_w[2]], axis=0)

    arrived = exchange(packed, folds)

    column = jnp.concatenate([early] + [shift(early, "y", by) for by in range(1, planes)], axis=0)
    column = jnp.concatenate([column, shift(column, "core", 1)], axis=0)
    shared_part = down(hidden_of(column, s_gate, s_up), s_down)
    rows = planes * own
    back = shift(shared_part[rows:].astype(jnp.bfloat16), "core", 1)
    shared_part = (shared_part[:rows] + back.astype(jnp.float32)).reshape(planes, own, width)
    shared = shared_part[0]
    for by in range(1, planes):
        back = shift(shared_part[by].astype(jnp.bfloat16), "y", planes - by)
        shared = shared + back.astype(jnp.float32)

    gate_w, up_w, down_w = lax.optimization_barrier((gate_w, up_w, down_w))

    mine = arrived.reshape(slots, width)
    left, right = shift(mine, "y", 1), shift(mine, "y", planes - 1)
    far = [shift(left[:half], "y", 1), shift(right[half:], "y", planes - 1)]
    far = jnp.concatenate(far, axis=0)

    total = down(hidden_of(mine, gate_w, up_w), down_w)
    near = hidden_of(jnp.concatenate([left[:half], right[half:], left[half:], right[:half]], axis=0), gate_w, up_w)
    free = down(near[:slots], down_w).astype(jnp.bfloat16)
    held = down(near[slots:], down_w)
    free = shift(free[half:], "y", 1), shift(free[:half], "y", planes - 1)
    far = down(hidden_of(far, gate_w, up_w), down_w).astype(jnp.bfloat16)
    far = shift(far[:half], "y", 1), shift(far[half:], "y", planes - 1)
    upper = (held[half:] + far[0].astype(jnp.float32)).astype(jnp.bfloat16)
    sent = shift(upper, "y", 1)
    upper, last = lax.optimization_barrier((upper, far[1]))
    lower = (held[:half] + last.astype(jnp.float32)).astype(jnp.bfloat16)
    held = sent, shift(lower, "y", planes - 1)
    back = (held[0], free[1]), (free[0], held[1])
    back = [sum(value.astype(jnp.float32) for value in values) for values in back]
    total = total + jnp.concatenate(back, axis=0)
    returned = exchange(total.astype(jnp.bfloat16), folds)

    return combine_rows(places, gates, shared, returned)


def solution(mesh):
    fine = Mesh(mesh.devices.reshape(4, 2, 4, 8), ("y", "core", "x", "z"))
    dp, expert = ("y", "core"), ("x", "z")
    placed = (
        P(dp + expert, None),
        P(dp + expert, None),
        P(dp + expert, None),
        P(expert, None, dp),
        P(expert, None, dp),
        P(expert, dp, None),
        P(None, dp),
        P(None, dp),
        P(dp, None),
    )
    return jax.shard_map(layer, mesh=fine, in_specs=placed, out_specs=P(dp + expert, None), check_vma=False)
```
